32 devices in a mesh: groups: 2 (over y), strip: 4 (over z), section: 2 (over x), col: 2 (over core).
Axes of the slice: x: 2, y: 2, z: 4, core: 2. Of those that a mesh axis runs over, the one named last changes fastest.
Arguments:
- x_in: float32 [8, 512, 16, 256], P('groups', None, 'strip', 'col'), parts along dimension 0, may hold values from -6 to 6
- w_reduce: float32 [2, 128, 512], P('section'), may hold values from -0.25 to 0.25
- w_spatial: float32 [2, 9, 128, 128], P('section'), may hold values from -0.1875 to 0.1875
- w_expand: float32 [2, 512, 128], P('section'), may hold values from -0.5 to 0.5
- gain_mid: float32 [2, 2, 128], P('section'), may hold values from 0.1 to 1.9
- bias_mid: float32 [2, 2, 128], P('section'), may hold values from -3 to 3
- gain_out: float32 [2, 512], P('section'), may hold values from 0.1 to 1.9
- bias_out: float32 [2, 512], P('section'), may hold values from -3 to 3
Outputs:
- features: float32 [2, 8, 512, 16, 256], P('section', 'groups', None, 'strip', 'col'), parts along dimension 1
The draws below stay inside these ranges and needn't reach their ends.
There are 2 independent parts, one for each index of `groups`. The reference program is written for one: setup_inputs(seed, part) draws one part's arguments, and reference() takes and returns one part's arrays. A program takes and returns all parts, laid end to end along the dimension named above; an argument that names none is the same for every part. Nothing has to cross between parts.
All inputs are finite; a program needn't handle non-finite values.
Results may differ from the reference program's by a relative error of at most 0.00015.
Values sent between devices are 32-bit elements; how exact they have to be, the bound alone decides.
A program may use at most 64 MiB of HBM per device.

```python
import jax
import jax.numpy as jnp
from jax import lax

C = 512
CM = 128
MB = 4
BLOCKS = 2
H = 16
W = 256


def block_levels(key, shape, cuts, low, high):
    factor_of, own = 1.0, jax.random.fold_in(key, 6)
    for axis_at, parts in cuts:
        heights = jnp.exp(jax.random.uniform(jax.random.fold_in(own, axis_at), (parts,), jnp.float32, low / len(cuts), high / len(cuts)))
        factor_of = factor_of * jnp.repeat(heights, shape[axis_at] // parts).reshape([-1 if axis == axis_at else 1 for axis in range(len(shape))])
    return factor_of


def centred(own_key, dims, spread, reach, split=(), dtype=jnp.bfloat16):
    factor_of = block_levels(own_key, dims, split, -0.22, 0.18) if split else 1.0
    drawn = jax.random.normal(own_key, dims, jnp.float32) * spread * factor_of
    return jnp.minimum(jnp.maximum(drawn, -reach), reach).astype(dtype)


def setup_inputs(seed: int = 0, part: int = 0) -> dict:
    key_of = jax.random.split(jax.random.key(seed), 9)
    part_keys = jax.random.split(jax.random.fold_in(key_of[8], part), 9)
    return {
        "x_in": centred(part_keys[0], (MB, C, H, W), 1.0, 6.0, ((2, 4), (3, 2)), jnp.float32),
        "w_reduce": centred(key_of[1], (BLOCKS, CM, C), C ** -0.5, 0.25, ((0, 2),), jnp.float32),
        "w_spatial": centred(key_of[2], (BLOCKS, 9, CM, CM), (9 * CM) ** -0.5, 0.1875, ((0, 2),), jnp.float32),
        "w_expand": centred(key_of[3], (BLOCKS, C, CM), CM ** -0.5, 0.5, ((0, 2),), jnp.float32),
        "gain_mid": jnp.clip(1.0 + 0.18 * jax.random.normal(key_of[4], (BLOCKS, 2, CM), jnp.float32), 0.1, 1.9),
        "bias_mid": centred(key_of[5], (BLOCKS, 2, CM), 0.5, 3.0, ((0, 2),), jnp.float32),
        "gain_out": jnp.clip(1.0 + 0.18 * jax.random.normal(key_of[6], (BLOCKS, C), jnp.float32), 0.1, 1.9),
        "bias_out": centred(key_of[7], (BLOCKS, C), 0.5, 3.0, ((0, 2),), jnp.float32),
    }


def project(weight, field):
    return jnp.einsum("oc,chw->ohw", weight, field, precision=lax.Precision.HIGHEST)


def column(vector):
    return vector[:, None, None]


def bottleneck(image, w_reduce, w_spatial, w_expand, gain_mid, bias_mid, gain_out, bias_out):
    reduced = jax.nn.relu(column(gain_mid[0]) * project(w_reduce, image) + column(bias_mid[0]))
    padded = jnp.pad(reduced, ((0, 0), (1, 1), (1, 1)))
    spatial = jnp.zeros((CM, H, W), jnp.float32)
    for tap in range(9):
        row_off = tap // 3
        col_off = tap % 3
        spatial = spatial + project(w_spatial[tap], padded[:, row_off:row_off + H, col_off:col_off + W])
    middle = jax.nn.relu(column(gain_mid[1]) * spatial + column(bias_mid[1]))
    return jax.nn.relu(image + column(gain_out) * project(w_expand, middle) + column(bias_out))


def reference(x_in, w_reduce, w_spatial, w_expand, gain_mid, bias_mid, gain_out, bias_out):
    def run_tile(image):
        outputs = []
        current = image
        for level in range(BLOCKS):
            current = bottleneck(current, w_reduce[level], w_spatial[level], w_expand[level],
                                 gain_mid[level], bias_mid[level], gain_out[level], bias_out[level])
            outputs.append(current)
        return jnp.stack(outputs)

    per_tile = lax.map(run_tile, x_in)
    return jnp.transpose(per_tile, (1, 0, 2, 3, 4))
```

```python
import functools

import jax
import jax.numpy as jnp
from jax import lax
from jax.experimental import pallas as pl
from jax.experimental.pallas import tpu as pltpu
from jax.sharding import PartitionSpec as P

BF = jnp.bfloat16
F32 = jnp.float32


def split(value):
    high = value.astype(BF)
    return high, (value - high.astype(F32)).astype(BF)


def dot(a, b):
    return jnp.dot(a, b, preferred_element_type=F32)


def down_rows(row, size):
    return jnp.transpose(jnp.broadcast_to(row, (size, size)))


def kernel(
    levels, strips, rows,
    x_ref, wr_ref, ws_ref, wx_ref, gm_ref, bm_ref, go_ref, bo_ref, cur,
    wr_all, ws_all, wx_all, pp_all, red, side, halo, relay,
    w_red, w_spa, w_exp, b_red, b_mid, b_out, sa,
    x_sem, own_sem, wsend, wrecv, rsend, rrecv, hsend, hrecv, nsend, nrecv, ysend, yrecv,
):
    tiles = x_ref.shape[0]
    chans = x_ref.shape[1] // rows
    cols = x_ref.shape[2]
    mid = wr_ref.shape[0]
    strip = lax.axis_index("strip")
    sec = lax.axis_index("section")
    col = lax.axis_index("col")
    other = {"col": 1 - col}
    srcs = (wr_ref, ws_ref, wx_ref)
    count = chans // mid
    terms = ((gm_ref, 0, 2), (bm_ref, 2, 2), (go_ref, 4, count), (bo_ref, 4 + count, count))
    slots = (wr_all, ws_all, wx_all, pp_all)

    def share(kind, level, which):
        if kind == 0:
            return wr_all.at[level, pl.ds(which * (mid // 2), mid // 2), :]
        if kind == 1:
            return ws_all.at[level, :, pl.ds(which * (mid // 2), mid // 2), :]
        if kind == 2:
            return wx_all.at[level, pl.ds(which * (chans // 2), chans // 2), :]
        return pp_all.at[level]

    def remote(src, dst, send, recv, device):
        return pltpu.make_async_remote_copy(
            src_ref=src, dst_ref=dst, send_sem=send, recv_sem=recv,
            device_id=device, device_id_type=pl.DeviceIdType.MESH,
        )

    own = [
        pltpu.make_async_copy(srcs[k], slots[k].at[sec], own_sem.at[k]) for k in range(3)
    ] + [
        [
            pltpu.make_async_copy(src, pp_all.at[sec, pl.ds(first, size), :], own_sem.at[3 + i])
            for i, (src, first, size) in enumerate(terms)
        ]
    ]
    loads = [
        pltpu.make_async_copy(x_ref.at[m], cur.at[m], x_sem.at[m]) for m in range(tiles)
    ]
    for copy in (*own[3], own[0], own[1], own[2]):
        copy.start()
    for copy in loads:
        copy.start()

    barrier = pltpu.get_barrier_semaphore()
    pl.semaphore_signal(barrier, inc=1, device_id=other, device_id_type=pl.DeviceIdType.MESH)
    for step in range(1, levels):
        pl.semaphore_signal(
            barrier, inc=1, device_id={"section": lax.rem(sec + step, levels)},
            device_id_type=pl.DeviceIdType.MESH,
        )

    for there, peer in ((strip > 0, strip - 1), (strip < strips - 1, strip + 1)):
        @pl.when(there)
        def _(peer=peer):
            pl.semaphore_signal(
                barrier, inc=1, device_id={"strip": peer}, device_id_type=pl.DeviceIdType.MESH
            )

    peers = levels + jnp.where(strip > 0, 1, 0) + jnp.where(strip < strips - 1, 1, 0)
    pl.semaphore_wait(barrier, peers)

    for k in (3, 0, 1, 2):
        for copy in own[3] if k == 3 else (own[k],):
            copy.wait()
        for target in range(1, levels):
            @pl.when(sec < target)
            def _(k=k, target=target):
                part = share(k, sec, col)
                remote(part, part, wsend.at[k, target], wrecv.at[k, sec], {"section": target}).start()

    @pl.when(strip == 0)
    def _():
        halo[:, :, 0] = jnp.zeros(halo.shape[:2] + halo.shape[3:], F32)
        relay[:, :, 0] = jnp.zeros(relay.shape[:2] + relay.shape[3:], F32)

    @pl.when(strip == strips - 1)
    def _():
        halo[:, :, 1] = jnp.zeros(halo.shape[:2] + halo.shape[3:], F32)
        relay[:, :, 1] = jnp.zeros(relay.shape[:2] + relay.shape[3:], F32)

    def relayed(k, level, which):
        part = share(k, level, which)
        return remote(part, part, rsend.at[k, level], rrecv.at[k, level], other)

    def arrive(level, kinds):
        @pl.when(sec > level)
        def _():
            for k in kinds:
                part = share(k, level, col)
                remote(part, part, wsend.at[k, 0], wrecv.at[k, level], other).wait_recv()
                if k < 3:
                    relayed(k, level, col).start()
            for k in kinds:
                if k < 3:
                    relayed(k, level, 1 - col).wait_recv()

    def prepare_reduce(level):
        arrive(level, (3, 0))
        gain = down_rows(pp_all[level, 0:1, :], mid)
        for at in range(chans // mid):
            cut = slice(at * mid, (at + 1) * mid)
            high, low = split(wr_all[level, :, cut] * gain)
            w_red[level, 0:mid, cut] = high
            w_red[level, mid : 2 * mid, cut] = low
        b_red[level] = down_rows(pp_all[level, 2:3, :], mid)

    def prepare_rest(level):
        arrive(level, (1, 2))
        gain = down_rows(pp_all[level, 1:2, :], mid)
        for tap in range(9):
            p, q = tap // 3, tap % 3
            high, low = split(ws_all[level, tap] * gain)
            w_spa[p, 0:mid, q * mid : (q + 1) * mid] = high
            w_spa[p, mid : 2 * mid, q * mid : (q + 1) * mid] = low
        b_mid[...] = down_rows(pp_all[level, 3:4, :], mid)
        for at in range(count):
            cut = slice(at * mid, (at + 1) * mid)
            high, low = split(wx_all[level, cut, :] * down_rows(pp_all[level, 4 + at : 5 + at, :], mid))
            w_exp[cut, 0:mid] = high
            w_exp[cut, mid : 2 * mid] = high
            w_exp[cut, 2 * mid : 3 * mid] = low
            b_out[cut, :] = down_rows(pp_all[level, 4 + count + at : 5 + count + at, :], mid)

    def to_strip(level, m, way):
        return remote(
            red.at[level, m, rows - 1 if way == 0 else 0], halo.at[level, m, way],
            hsend.at[level, m, way], hrecv.at[level, m, way],
            {"strip": strip + 1 if way == 0 else strip - 1},
        )

    def to_side(level, m):
        return remote(red.at[level, m], side.at[level, m], nsend.at[level, m], nrecv.at[level, m], other)

    def pass_on(level, m, way):
        return remote(
            halo.at[level, m, way], relay.at[level, m, way],
            ysend.at[level, m, way], yrecv.at[level, m, way], other,
        )

    has = (strip > 0, strip < strips - 1)

    def reduce_tile(level, m):
        weights = w_red[level]
        bias = b_red[level]
        for pair in range(rows // 2):
            parts = [
                split(cur.at[m][pl.ds(2 * pair + j, chans, stride=rows), :]) for j in range(2)
            ]
            high = jnp.concatenate([part[0] for part in parts], axis=1)
            low = jnp.concatenate([part[1] for part in parts], axis=1)
            both = dot(weights, high)
            total = both[:mid] + both[mid:] + dot(weights[:mid], low)
            for j in range(2):
                red[level, m, 2 * pair + j] = jnp.maximum(total[:, j * cols : (j + 1) * cols] + bias, 0.0)

        @pl.when(has[1])
        def _():
            to_strip(level, m, 0).start()

        @pl.when(has[0])
        def _():
            to_strip(level, m, 1).start()

        to_side(level, m).start()

    def take_halo(level, m):
        for way in range(2):
            @pl.when(has[way])
            def _(way=way):
                to_strip(level, m, way).wait_recv()
                pass_on(level, m, way).start()

    lane = lax.broadcasted_iota(jnp.int32, (mid, cols), 1)
    left_edge = lane == cols - 1
    right_edge = lane == 0
    left_on = jnp.where(col == 1, 1.0, 0.0).astype(F32)
    right_on = jnp.where(col == 0, 1.0, 0.0).astype(F32)

    def finish_tile(level, m):
        to_side(level, m).wait_recv()
        for way in range(2):
            @pl.when(has[way])
            def _(way=way):
                pass_on(level, m, way).wait_recv()
        for at in range(rows + 2):
            if at == 0:
                centre, beside = halo[level, m, 0], relay[level, m, 0]
            elif at == rows + 1:
                centre, beside = halo[level, m, 1], relay[level, m, 1]
            else:
                centre, beside = red[level, m, at - 1], side[level, m, at - 1]
            lanes = slice(at * cols, (at + 1) * cols)
            left = pltpu.roll(jnp.where(left_edge, beside * left_on, centre), 1, 1)
            right = pltpu.roll(jnp.where(right_edge, beside * right_on, centre), cols - 1, 1)
            for q, value in enumerate((left, centre, right)):
                high, low = split(value)
                sa[q * mid : (q + 1) * mid, lanes] = high
                sa[(3 + q) * mid : (4 + q) * mid, lanes] = low
        bias = b_mid[...]
        for pair in range(rows // 2):
            both = jnp.zeros((2 * mid, 2 * cols), F32)
            one = jnp.zeros((mid, 2 * cols), F32)
            for p in range(3):
                lanes = slice((2 * pair + p) * cols, (2 * pair + p + 2) * cols)
                both = both + dot(w_spa[p], sa[0 : 3 * mid, lanes])
                one = one + dot(w_spa[p, 0:mid, :], sa[3 * mid : 6 * mid, lanes])
            total = both[:mid] + both[mid:] + one
            total = jnp.maximum(total + jnp.concatenate([bias, bias], axis=1), 0.0)
            high, low = split(total)
            stack = jnp.concatenate([high, low, high], axis=0)
            grown = dot(w_exp[...], stack)
            for j in range(2):
                at = pl.ds(2 * pair + j, chans, stride=rows)
                cur.at[m][at, :] = jnp.maximum(
                    cur.at[m][at, :] + grown[:, j * cols : (j + 1) * cols] + b_out[...], 0.0
                )

    prepare_reduce(0)

    @pl.loop(0, tiles)
    def _(m):
        pltpu.make_async_copy(x_ref.at[m], cur.at[m], x_sem.at[m]).wait()
        reduce_tile(0, m)

    for level in range(levels):
        @pl.when(sec >= level)
        def _(level=level):
            prepare_rest(level)
            if level + 1 < levels:
                @pl.when(sec > level)
                def _():
                    prepare_reduce(level + 1)

            take_halo(level, 0)

            @pl.loop(0, tiles)
            def _(m):
                @pl.when(m + 1 < tiles)
                def _():
                    take_halo(level, m + 1)

                finish_tile(level, m)
                if level + 1 < levels:
                    @pl.when(sec > level)
                    def _():
                        reduce_tile(level + 1, m)

            @pl.loop(0, tiles)
            def _(m):
                to_side(level, m).wait_send()
                for way in range(2):
                    @pl.when(has[1 - way])
                    def _(way=way):
                        to_strip(level, m, way).wait_send()

                    @pl.when(has[way])
                    def _(way=way):
                        pass_on(level, m, way).wait_send()

    for k in range(4):
        for target in range(1, levels):
            @pl.when(sec < target)
            def _(k=k, target=target):
                part = share(k, sec, col)
                remote(part, part, wsend.at[k, target], wrecv.at[k, sec], {"section": target}).wait_send()
        if k < 3:
            for level in range(levels - 1):
                @pl.when(sec > level)
                def _(k=k, level=level):
                    relayed(k, level, col).wait_send()


def on_device(levels, strips, x_in, w_reduce, w_spatial, w_expand, gain_mid, bias_mid, gain_out, bias_out):
    tiles, chans, rows, cols = x_in.shape
    mid = w_reduce.shape[1]
    dma = pltpu.SemaphoreType.DMA
    out = pl.pallas_call(
        functools.partial(kernel, levels, strips, rows),
        out_shape=jax.ShapeDtypeStruct((tiles, chans * rows, cols), F32),
        in_specs=[pl.BlockSpec(memory_space=pl.ANY)] * 8,
        out_specs=pl.BlockSpec(memory_space=pltpu.VMEM),
        scratch_shapes=[
            pltpu.VMEM((levels, mid, chans), F32),
            pltpu.VMEM((levels, 9, mid, mid), F32),
            pltpu.VMEM((levels, chans, mid), F32),
            pltpu.VMEM((levels, 4 + 2 * (chans // mid), mid), F32),
            pltpu.VMEM((levels, tiles, rows, mid, cols), F32),
            pltpu.VMEM((levels, tiles, rows, mid, cols), F32),
            pltpu.VMEM((levels, tiles, 2, mid, cols), F32),
            pltpu.VMEM((levels, tiles, 2, mid, cols), F32),
            pltpu.VMEM((levels, 2 * mid, chans), BF),
            pltpu.VMEM((3, 2 * mid, 3 * mid), BF),
            pltpu.VMEM((chans, 3 * mid), BF),
            pltpu.VMEM((levels, mid, cols), F32),
            pltpu.VMEM((mid, cols), F32),
            pltpu.VMEM((chans, cols), F32),
            pltpu.VMEM((6 * mid, (rows + 2) * cols), BF),
            dma((tiles,)),
            dma((7,)),
            dma((4, levels)),
            dma((4, levels)),
            dma((3, levels)),
            dma((3, levels)),
            dma((levels, tiles, 2)),
            dma((levels, tiles, 2)),
            dma((levels, tiles)),
            dma((levels, tiles)),
            dma((levels, tiles, 2)),
            dma((levels, tiles, 2)),
        ],
        compiler_params=pltpu.CompilerParams(
            collective_id=0, has_side_effects=True, vmem_limit_bytes=40 * 1024 * 1024
        ),
        name="blocks",
    )(x_in.reshape(tiles, chans * rows, cols), w_reduce[0], w_spatial[0], w_expand[0],
      gain_mid[0], bias_mid[0], gain_out.reshape(chans // mid, mid), bias_out.reshape(chans // mid, mid))
    return out.reshape(1, tiles, chans, rows, cols)


def solution(mesh):
    in_specs = (
        P("groups", None, "strip", "col"),
        P("section", None, None),
        P("section", None, None, None),
        P("section", None, None),
        P("section", None, None),
        P("section", None, None),
        P("section", None),
        P("section", None),
    )
    out_specs = P("section", "groups", None, "strip", "col")
    return jax.shard_map(
        functools.partial(on_device, mesh.shape["section"], mesh.shape["strip"]),
        mesh=mesh, in_specs=in_specs, out_specs=out_specs, check_vma=False,
    )
```

```python
import functools

import jax
import jax.numpy as jnp
from jax import lax
from jax.experimental import pallas as pl
from jax.experimental.pallas import tpu as pltpu
from jax.sharding import PartitionSpec as P

BF = jnp.bfloat16
F32 = jnp.float32


def split(value):
    high = value.astype(BF)
    return high, (value - high.astype(F32)).astype(BF)


def dot(a, b):
    return jnp.dot(a, b, preferred_element_type=F32)


def down_rows(row, size):
    return jnp.transpose(jnp.broadcast_to(row, (size, size)))


def kernel(
    levels, strips, rows,
    x_ref, wr_ref, ws_ref, wx_ref, gm_ref, bm_ref, go_ref, bo_ref, cur,
    wr_all, ws_all, wx_all, pp_all, red, side, halo, relay,
    w_red, w_spa, w_exp, b_red, b_mid, b_out, sa, middle,
    x_sem, own_sem, wsend, wrecv, rsend, rrecv, hsend, hrecv, nsend, nrecv, ysend, yrecv,
):
    tiles = x_ref.shape[0]
    chans = x_ref.shape[1] // rows
    cols = x_ref.shape[2]
    mid = wr_ref.shape[0]
    strip = lax.axis_index("strip")
    sec = lax.axis_index("section")
    col = lax.axis_index("col")
    other = {"col": 1 - col}
    srcs = (wr_ref, ws_ref, wx_ref)
    count = chans // mid
    terms = ((gm_ref, 0, 2), (bm_ref, 2, 2), (go_ref, 4, count), (bo_ref, 4 + count, count))
    slots = (wr_all, ws_all, wx_all, pp_all)

    def share(kind, level, which):
        if kind == 0:
            return wr_all.at[level, pl.ds(which * (mid // 2), mid // 2), :]
        if kind == 1:
            return ws_all.at[level, :, pl.ds(which * (mid // 2), mid // 2), :]
        if kind == 2:
            return wx_all.at[level, pl.ds(which * (chans // 2), chans // 2), :]
        return pp_all.at[level]

    def remote(src, dst, send, recv, device):
        return pltpu.make_async_remote_copy(
            src_ref=src, dst_ref=dst, send_sem=send, recv_sem=recv,
            device_id=device, device_id_type=pl.DeviceIdType.MESH,
        )

    own = [
        pltpu.make_async_copy(srcs[k], slots[k].at[sec], own_sem.at[k]) for k in range(3)
    ] + [
        [
            pltpu.make_async_copy(src, pp_all.at[sec, pl.ds(first, size), :], own_sem.at[3 + i])
            for i, (src, first, size) in enumerate(terms)
        ]
    ]
    loads = [
        pltpu.make_async_copy(x_ref.at[m], cur.at[m], x_sem.at[m]) for m in range(tiles)
    ]
    for copy in (*own[3], own[0], own[1], own[2]):
        copy.start()
    for copy in loads:
        copy.start()

    barrier = pltpu.get_barrier_semaphore()
    pl.semaphore_signal(barrier, inc=1, device_id=other, device_id_type=pl.DeviceIdType.MESH)
    for step in range(1, levels):
        pl.semaphore_signal(
            barrier, inc=1, device_id={"section": lax.rem(sec + step, levels)},
            device_id_type=pl.DeviceIdType.MESH,
        )

    for there, peer in ((strip > 0, strip - 1), (strip < strips - 1, strip + 1)):
        @pl.when(there)
        def _(peer=peer):
            pl.semaphore_signal(
                barrier, inc=1, device_id={"strip": peer}, device_id_type=pl.DeviceIdType.MESH
            )

    peers = levels + jnp.where(strip > 0, 1, 0) + jnp.where(strip < strips - 1, 1, 0)
    pl.semaphore_wait(barrier, peers)

    for k in (3, 0, 1, 2):
        for copy in own[3] if k == 3 else (own[k],):
            copy.wait()
        for target in range(1, levels):
            @pl.when(sec < target)
            def _(k=k, target=target):
                part = share(k, sec, col)
                remote(part, part, wsend.at[k, target], wrecv.at[k, sec], {"section": target}).start()

    @pl.when(strip == 0)
    def _():
        halo[:, :, 0] = jnp.zeros(halo.shape[:2] + halo.shape[3:], F32)
        relay[:, :, 0] = jnp.zeros(relay.shape[:2] + relay.shape[3:], F32)

    @pl.when(strip == strips - 1)
    def _():
        halo[:, :, 1] = jnp.zeros(halo.shape[:2] + halo.shape[3:], F32)
        relay[:, :, 1] = jnp.zeros(relay.shape[:2] + relay.shape[3:], F32)

    def relayed(k, level, which):
        part = share(k, level, which)
        return remote(part, part, rsend.at[k, level], rrecv.at[k, level], other)

    def arrive(level, kinds):
        @pl.when(sec > level)
        def _():
            for k in kinds:
                part = share(k, level, col)
                remote(part, part, wsend.at[k, 0], wrecv.at[k, level], other).wait_recv()
                if k < 3:
                    relayed(k, level, col).start()
            for k in kinds:
                if k < 3:
                    relayed(k, level, 1 - col).wait_recv()

    def prepare_reduce(level):
        arrive(level, (3, 0))
        gain = down_rows(pp_all[level, 0:1, :], mid)
        for at in range(chans // mid):
            cut = slice(at * mid, (at + 1) * mid)
            high, low = split(wr_all[level, :, cut] * gain)
            w_red[level, 0:mid, cut] = high
            w_red[level, mid : 2 * mid, cut] = low
        b_red[level] = down_rows(pp_all[level, 2:3, :], mid)

    def prepare_rest(level):
        arrive(level, (1, 2))
        gain = down_rows(pp_all[level, 1:2, :], mid)
        for tap in range(9):
            high, low = split(ws_all[level, tap] * gain)
            w_spa[0:mid, tap * mid : (tap + 1) * mid] = high
            w_spa[mid : 2 * mid, tap * mid : (tap + 1) * mid] = low
        b_mid[...] = down_rows(pp_all[level, 3:4, :], mid)
        for at in range(count):
            cut = slice(at * mid, (at + 1) * mid)
            high, low = split(wx_all[level, cut, :] * down_rows(pp_all[level, 4 + at : 5 + at, :], mid))
            w_exp[cut, 0:mid] = high
            w_exp[cut, mid : 2 * mid] = high
            w_exp[cut, 2 * mid : 3 * mid] = low
            b_out[cut, :] = down_rows(pp_all[level, 4 + count + at : 5 + count + at, :], mid)

    def to_strip(level, m, way):
        return remote(
            red.at[level, m, rows - 1 if way == 0 else 0], halo.at[level, m, way],
            hsend.at[level, m, way], hrecv.at[level, m, way],
            {"strip": strip + 1 if way == 0 else strip - 1},
        )

    def to_side(level, m):
        return remote(red.at[level, m], side.at[level, m], nsend.at[level, m], nrecv.at[level, m], other)

    def pass_on(level, m, way):
        return remote(
            halo.at[level, m, way], relay.at[level, m, way],
            ysend.at[level, m, way], yrecv.at[level, m, way], other,
        )

    has = (strip > 0, strip < strips - 1)

    def reduce_tile(level, m):
        weights = w_red[level]
        bias = b_red[level]
        for pair in range(rows // 2):
            parts = [
                split(cur.at[m][pl.ds(2 * pair + j, chans, stride=rows), :]) for j in range(2)
            ]
            high = jnp.concatenate([part[0] for part in parts], axis=1)
            low = jnp.concatenate([part[1] for part in parts], axis=1)
            both = dot(weights, high)
            total = both[:mid] + both[mid:] + dot(weights[:mid], low)
            for j in range(2):
                red[level, m, 2 * pair + j] = jnp.maximum(total[:, j * cols : (j + 1) * cols] + bias, 0.0)

        @pl.when(has[1])
        def _():
            to_strip(level, m, 0).start()

        @pl.when(has[0])
        def _():
            to_strip(level, m, 1).start()

        to_side(level, m).start()

    def take_halo(level, m):
        for way in range(2):
            @pl.when(has[way])
            def _(way=way):
                to_strip(level, m, way).wait_recv()
                pass_on(level, m, way).start()

    lane = lax.broadcasted_iota(jnp.int32, (mid, cols), 1)
    left_edge = lane == cols - 1
    right_edge = lane == 0
    left_on = jnp.where(col == 1, 1.0, 0.0).astype(F32)
    right_on = jnp.where(col == 0, 1.0, 0.0).astype(F32)

    def finish_tile(level, m):
        to_side(level, m).wait_recv()
        for way in range(2):
            @pl.when(has[way])
            def _(way=way):
                pass_on(level, m, way).wait_recv()
        for at in range(rows + 2):
            if at == 0:
                centre, beside = halo[level, m, 0], relay[level, m, 0]
            elif at == rows + 1:
                centre, beside = halo[level, m, 1], relay[level, m, 1]
            else:
                centre, beside = red[level, m, at - 1], side[level, m, at - 1]
            lanes = slice(at * cols, (at + 1) * cols)
            left = pltpu.roll(jnp.where(left_edge, beside * left_on, centre), 1, 1)
            right = pltpu.roll(jnp.where(right_edge, beside * right_on, centre), cols - 1, 1)
            for q, value in enumerate((left, centre, right)):
                high, low = split(value)
                sa[q * mid : (q + 1) * mid, lanes] = high
                sa[(3 + q) * mid : (4 + q) * mid, lanes] = low
        wide = rows * cols
        high, low = (
            jnp.concatenate(
                [sa[first : first + 3 * mid, p * cols : p * cols + wide] for p in range(3)], axis=0
            )
            for first in (0, 3 * mid)
        )
        both = dot(w_spa[...], high)
        total = both[:mid] + both[mid:] + dot(w_spa[0:mid, :], low)
        total = jnp.maximum(total + jnp.concatenate([b_mid[...]] * rows, axis=1), 0.0)
        high, low = split(total)
        middle[0:mid, :] = high
        middle[mid : 2 * mid, :] = low
        for pair in range(rows // 2):
            lanes = slice(2 * pair * cols, (2 * pair + 2) * cols)
            high, low = middle[0:mid, lanes], middle[mid : 2 * mid, lanes]
            grown = dot(w_exp[...], jnp.concatenate([high, low, high], axis=0))
            for j in range(2):
                at = pl.ds(2 * pair + j, chans, stride=rows)
                cur.at[m][at, :] = jnp.maximum(
                    cur.at[m][at, :] + grown[:, j * cols : (j + 1) * cols] + b_out[...], 0.0
                )

    prepare_reduce(0)

    @pl.loop(0, tiles)
    def _(m):
        pltpu.make_async_copy(x_ref.at[m], cur.at[m], x_sem.at[m]).wait()
        reduce_tile(0, m)

    for level in range(levels):
        @pl.when(sec >= level)
        def _(level=level):
            prepare_rest(level)
            if level + 1 < levels:
                @pl.when(sec > level)
                def _():
                    prepare_reduce(level + 1)

            take_halo(level, 0)

            @pl.loop(0, tiles)
            def _(m):
                @pl.when(m + 1 < tiles)
                def _():
                    take_halo(level, m + 1)

                finish_tile(level, m)
                if level + 1 < levels:
                    @pl.when(sec > level)
                    def _():
                        reduce_tile(level + 1, m)

            @pl.loop(0, tiles)
            def _(m):
                to_side(level, m).wait_send()
                for way in range(2):
                    @pl.when(has[1 - way])
                    def _(way=way):
                        to_strip(level, m, way).wait_send()

                    @pl.when(has[way])
                    def _(way=way):
                        pass_on(level, m, way).wait_send()

    for k in range(4):
        for target in range(1, levels):
            @pl.when(sec < target)
            def _(k=k, target=target):
                part = share(k, sec, col)
                remote(part, part, wsend.at[k, target], wrecv.at[k, sec], {"section": target}).wait_send()
        if k < 3:
            for level in range(levels - 1):
                @pl.when(sec > level)
                def _(k=k, level=level):
                    relayed(k, level, col).wait_send()


def on_device(levels, strips, x_in, w_reduce, w_spatial, w_expand, gain_mid, bias_mid, gain_out, bias_out):
    tiles, chans, rows, cols = x_in.shape
    mid = w_reduce.shape[1]
    operands = (
        x_in.reshape(tiles, chans * rows, cols), w_reduce[0], w_spatial[0], w_expand[0],
        gain_mid[0], bias_mid[0], gain_out.reshape(chans // mid, mid), bias_out.reshape(chans // mid, mid),
    )
    dma = pltpu.SemaphoreType.DMA
    out = pl.pallas_call(
        functools.partial(kernel, levels, strips, rows),
        out_shape=jax.ShapeDtypeStruct((tiles, chans * rows, cols), F32),
        in_specs=[pl.BlockSpec(memory_space=pltpu.HBM)] * 8,
        out_specs=pl.BlockSpec(memory_space=pltpu.VMEM),
        scratch_shapes=[
            pltpu.VMEM((levels, mid, chans), F32),
            pltpu.VMEM((levels, 9, mid, mid), F32),
            pltpu.VMEM((levels, chans, mid), F32),
            pltpu.VMEM((levels, 4 + 2 * (chans // mid), mid), F32),
            pltpu.VMEM((levels, tiles, rows, mid, cols), F32),
            pltpu.VMEM((levels, tiles, rows, mid, cols), F32),
            pltpu.VMEM((levels, tiles, 2, mid, cols), F32),
            pltpu.VMEM((levels, tiles, 2, mid, cols), F32),
            pltpu.VMEM((levels, 2 * mid, chans), BF),
            pltpu.VMEM((2 * mid, 9 * mid), BF),
            pltpu.VMEM((chans, 3 * mid), BF),
            pltpu.VMEM((levels, mid, cols), F32),
            pltpu.VMEM((mid, cols), F32),
            pltpu.VMEM((chans, cols), F32),
            pltpu.VMEM((6 * mid, (rows + 2) * cols), BF),
            pltpu.VMEM((2 * mid, rows * cols), BF),
            dma((tiles,)),
            dma((7,)),
            dma((4, levels)),
            dma((4, levels)),
            dma((3, levels)),
            dma((3, levels)),
            dma((levels, tiles, 2)),
            dma((levels, tiles, 2)),
            dma((levels, tiles)),
            dma((levels, tiles)),
            dma((levels, tiles, 2)),
            dma((levels, tiles, 2)),
        ],
        compiler_params=pltpu.CompilerParams(
            collective_id=0, has_side_effects=True, vmem_limit_bytes=40 * 1024 * 1024
        ),
        name="blocks",
    )(*(pltpu.with_memory_space_constraint(value, pltpu.HBM) for value in operands))
    return out.reshape(1, tiles, chans, rows, cols)


def solution(mesh):
    in_specs = (
        P("groups", None, "strip", "col"),
        P("section", None, None),
        P("section", None, None, None),
        P("section", None, None),
        P("section", None, None),
        P("section", None, None),
        P("section", None),
        P("section", None),
    )
    out_specs = P("section", "groups", None, "strip", "col")
    return jax.shard_map(
        functools.partial(on_device, mesh.shape["section"], mesh.shape["strip"]),
        mesh=mesh, in_specs=in_specs, out_specs=out_specs, check_vma=False,
    )
```

```python
import functools

import jax
import jax.numpy as jnp
from jax import lax
from jax.experimental import pallas as pl
from jax.experimental.pallas import tpu as pltpu
from jax.sharding import PartitionSpec as P

BF = jnp.bfloat16
F32 = jnp.float32


def split(value):
    high = value.astype(BF)
    return high, (value - high.astype(F32)).astype(BF)


def dot(a, b):
    return jnp.dot(a, b, preferred_element_type=F32)


def down_rows(row, size):
    return jnp.transpose(jnp.broadcast_to(row, (size, size)))


def kernel(
    levels, strips, groups, rows,
    x_ref, wr_ref, ws_ref, wx_ref, gm_ref, bm_ref, go_ref, bo_ref, cur,
    wr_all, ws_all, wx_all, pp_all, red, side, halo, relay,
    w_red, w_spa, w_exp, b_red, b_mid, b_out, sa, middle,
    x_sem, own_sem, wsend, wrecv, gsend, grecv, rsend, rrecv, hsend, hrecv, nsend, nrecv, ysend, yrecv,
):
    tiles = x_ref.shape[0]
    chans = x_ref.shape[1] // rows
    cols = x_ref.shape[2]
    mid = wr_ref.shape[0]
    strip = lax.axis_index("strip")
    sec = lax.axis_index("section")
    col = lax.axis_index("col")
    grp = lax.axis_index("groups")
    other = {"col": 1 - col}
    srcs = (wr_ref, ws_ref, wx_ref)
    count = chans // mid
    terms = ((gm_ref, 0, 2), (bm_ref, 2, 2), (go_ref, 4, count), (bo_ref, 4 + count, count))
    slots = (wr_all, ws_all, wx_all, pp_all)

    def share(piece, level, which, of):
        part = which * groups + of
        if piece == 0:
            size = mid // (2 * groups)
            return wr_all.at[level, pl.ds(part * size, size), :]
        if piece < 4:
            size = mid // (2 * groups)
            return ws_all.at[level, pl.ds(3 * (piece - 1), 3), pl.ds(part * size, size), :]
        if piece == 4:
            size = chans // (2 * groups)
            return wx_all.at[level, pl.ds(part * size, size), :]
        return pp_all.at[level]

    def remote(src, dst, send, recv, device):
        return pltpu.make_async_remote_copy(
            src_ref=src, dst_ref=dst, send_sem=send, recv_sem=recv,
            device_id=device, device_id_type=pl.DeviceIdType.MESH,
        )

    def across(piece, level, target):
        part = share(piece, level, col, grp)
        return remote(
            part, part, wsend.at[piece, target], wrecv.at[piece, level], {"section": target}
        )

    def to_group(piece, level, step):
        part = share(piece, level, col, grp)
        return remote(
            part, part, gsend.at[piece, level, step], grecv.at[piece, level, step],
            {"groups": lax.rem(grp + step, groups)},
        )

    def to_core(piece, level, which, step):
        part = share(piece, level, which, lax.rem(grp + groups - step, groups))
        return remote(part, part, rsend.at[piece, level, step], rrecv.at[piece, level, step], other)

    def forward(piece, level):
        across(piece, level, 0).wait_recv()
        if piece < 5:
            for step in range(1, groups):
                to_group(piece, level, step).start()
            to_core(piece, level, col, 0).start()

    def collect(piece, level):
        for step in range(1, groups):
            part = share(piece, level, col, lax.rem(grp + groups - step, groups))
            remote(
                part, part, gsend.at[piece, level, step], grecv.at[piece, level, step], other
            ).wait_recv()
            to_core(piece, level, col, step).start()

    def complete(piece, level):
        for step in range(groups):
            to_core(piece, level, 1 - col, step).wait_recv()

    own = [
        pltpu.make_async_copy(srcs[k], slots[k].at[sec], own_sem.at[k]) for k in range(3)
    ] + [
        [
            pltpu.make_async_copy(src, pp_all.at[sec, pl.ds(first, size), :], own_sem.at[3 + i])
            for i, (src, first, size) in enumerate(terms)
        ]
    ]
    loads = [
        pltpu.make_async_copy(x_ref.at[m], cur.at[m], x_sem.at[m]) for m in range(tiles)
    ]
    for copy in (*own[3], own[0], own[1], own[2]):
        copy.start()
    for copy in loads:
        copy.start()

    barrier = pltpu.get_barrier_semaphore()
    pl.semaphore_signal(barrier, inc=1, device_id=other, device_id_type=pl.DeviceIdType.MESH)
    for step in range(1, levels):
        pl.semaphore_signal(
            barrier, inc=1, device_id={"section": lax.rem(sec + step, levels)},
            device_id_type=pl.DeviceIdType.MESH,
        )

    for there, peer in ((strip > 0, strip - 1), (strip < strips - 1, strip + 1)):
        @pl.when(there)
        def _(peer=peer):
            pl.semaphore_signal(
                barrier, inc=1, device_id={"strip": peer}, device_id_type=pl.DeviceIdType.MESH
            )

    for step in range(1, groups):
        pl.semaphore_signal(
            barrier, inc=1, device_id={"groups": lax.rem(grp + step, groups)},
            device_id_type=pl.DeviceIdType.MESH,
        )

    peers = levels + groups - 1 + jnp.where(strip > 0, 1, 0) + jnp.where(strip < strips - 1, 1, 0)
    pl.semaphore_wait(barrier, peers)

    for piece in (5, 0, 1, 2, 3, 4):
        for copy in {5: own[3], 0: own[:1], 1: own[1:2], 4: own[2:3]}.get(piece, ()):
            copy.wait()
        for target in range(1, levels):
            @pl.when(sec < target)
            def _(piece=piece, target=target):
                across(piece, sec, target).start()

    @pl.when(strip == 0)
    def _():
        halo[:, :, 0] = jnp.zeros(halo.shape[:2] + halo.shape[3:], F32)
        relay[:, :, 0] = jnp.zeros(relay.shape[:2] + relay.shape[3:], F32)

    @pl.when(strip == strips - 1)
    def _():
        halo[:, :, 1] = jnp.zeros(halo.shape[:2] + halo.shape[3:], F32)
        relay[:, :, 1] = jnp.zeros(relay.shape[:2] + relay.shape[3:], F32)

    def prepare_reduce(level):
        gain = down_rows(pp_all[level, 0:1, :], mid)
        for at in range(count):
            cut = slice(at * mid, (at + 1) * mid)
            high, low = split(wr_all[level, :, cut] * gain)
            w_red[level, 0:mid, cut] = high
            w_red[level, mid : 2 * mid, cut] = low
        b_red[level] = down_rows(pp_all[level, 2:3, :], mid)

    def prepare_spatial(level):
        gain = down_rows(pp_all[level, 1:2, :], mid)
        for tap in range(9):
            high, low = split(ws_all[level, tap] * gain)
            w_spa[level, 0:mid, tap * mid : (tap + 1) * mid] = high
            w_spa[level, mid : 2 * mid, tap * mid : (tap + 1) * mid] = low
        b_mid[level] = down_rows(pp_all[level, 3:4, :], mid)

    def prepare_expand(level):
        for at in range(count):
            cut = slice(at * mid, (at + 1) * mid)
            high, low = split(wx_all[level, cut, :] * down_rows(pp_all[level, pl.ds(4 + at, 1), :], mid))
            w_exp[level, cut, 0:mid] = high
            w_exp[level, cut, mid : 2 * mid] = high
            w_exp[level, cut, 2 * mid : 3 * mid] = low
            b_out[level, cut, :] = down_rows(pp_all[level, pl.ds(4 + count + at, 1), :], mid)

    def arrive_reduce(level):
        for piece in (5, 0, 1, 2):
            forward(piece, level)
        collect(0, level)
        forward(3, level)
        complete(0, level)
        prepare_reduce(level)

    def arrive_rest(level):
        for piece in (1, 2, 3):
            collect(piece, level)
        for piece in (1, 2, 3):
            complete(piece, level)
        prepare_spatial(level)
        collect(4, level)
        complete(4, level)
        prepare_expand(level)

    def to_strip(level, m, way):
        return remote(
            red.at[level, m, rows - 1 if way == 0 else 0], halo.at[level, m, way],
            hsend.at[level, m, way], hrecv.at[level, m, way],
            {"strip": strip + 1 if way == 0 else strip - 1},
        )

    def to_side(level, m):
        return remote(red.at[level, m], side.at[level, m], nsend.at[level, m], nrecv.at[level, m], other)

    def pass_on(level, m, way):
        return remote(
            halo.at[level, m, way], relay.at[level, m, way],
            ysend.at[level, m, way], yrecv.at[level, m, way], other,
        )

    has = (strip > 0, strip < strips - 1)

    def reduce_tile(level, m):
        weights = w_red[level]
        bias = b_red[level]
        for pair in range(rows // 2):
            parts = [
                split(cur.at[m][pl.ds(2 * pair + j, chans, stride=rows), :]) for j in range(2)
            ]
            high = jnp.concatenate([part[0] for part in parts], axis=1)
            low = jnp.concatenate([part[1] for part in parts], axis=1)
            both = dot(weights, high)
            total = both[:mid] + both[mid:] + dot(weights[:mid], low)
            for j in range(2):
                red[level, m, 2 * pair + j] = jnp.maximum(total[:, j * cols : (j + 1) * cols] + bias, 0.0)

        @pl.when(has[1])
        def _():
            to_strip(level, m, 0).start()

        @pl.when(has[0])
        def _():
            to_strip(level, m, 1).start()

        to_side(level, m).start()

    def take_halo(level, m):
        for way in range(2):
            @pl.when(has[way])
            def _(way=way):
                to_strip(level, m, way).wait_recv()
                pass_on(level, m, way).start()

    lane = lax.broadcasted_iota(jnp.int32, (mid, cols), 1)
    left_edge = lane == cols - 1
    right_edge = lane == 0
    left_on = jnp.where(col == 1, 1.0, 0.0).astype(F32)
    right_on = jnp.where(col == 0, 1.0, 0.0).astype(F32)

    def finish_tile(level, m):
        to_side(level, m).wait_recv()
        for way in range(2):
            @pl.when(has[way])
            def _(way=way):
                pass_on(level, m, way).wait_recv()
        for at in range(rows + 2):
            if at == 0:
                centre, beside = halo[level, m, 0], relay[level, m, 0]
            elif at == rows + 1:
                centre, beside = halo[level, m, 1], relay[level, m, 1]
            else:
                centre, beside = red[level, m, at - 1], side[level, m, at - 1]
            lanes = slice(at * cols, (at + 1) * cols)
            left = pltpu.roll(jnp.where(left_edge, beside * left_on, centre), 1, 1)
            right = pltpu.roll(jnp.where(right_edge, beside * right_on, centre), cols - 1, 1)
            for q, value in enumerate((left, centre, right)):
                high, low = split(value)
                sa[q * mid : (q + 1) * mid, lanes] = high
                sa[(3 + q) * mid : (4 + q) * mid, lanes] = low
        wide = rows * cols
        high, low = (
            jnp.concatenate(
                [sa[first : first + 3 * mid, p * cols : p * cols + wide] for p in range(3)], axis=0
            )
            for first in (0, 3 * mid)
        )
        both = dot(w_spa[level], high)
        total = both[:mid] + both[mid:] + dot(w_spa[level, 0:mid, :], low)
        total = jnp.maximum(total + jnp.concatenate([b_mid[level]] * rows, axis=1), 0.0)
        high, low = split(total)
        middle[0:mid, :] = high
        middle[mid : 2 * mid, :] = low
        for pair in range(rows // 2):
            lanes = slice(2 * pair * cols, (2 * pair + 2) * cols)
            high, low = middle[0:mid, lanes], middle[mid : 2 * mid, lanes]
            grown = dot(w_exp[level], jnp.concatenate([high, low, high], axis=0))
            for j in range(2):
                at = pl.ds(2 * pair + j, chans, stride=rows)
                cur.at[m][at, :] = jnp.maximum(
                    cur.at[m][at, :] + grown[:, j * cols : (j + 1) * cols] + b_out[level], 0.0
                )

    prepare_reduce(sec)

    @pl.when(sec > 0)
    def _():
        prepare_spatial(sec)
        prepare_expand(sec)
        arrive_reduce(0)

    @pl.loop(0, tiles)
    def _(m):
        pltpu.make_async_copy(x_ref.at[m], cur.at[m], x_sem.at[m]).wait()
        reduce_tile(0, m)

        @pl.when((sec > 0) & (m == 0))
        def _():
            forward(4, 0)

    @pl.when(sec == 0)
    def _():
        prepare_spatial(0)
        prepare_expand(0)

    for level in range(levels):
        @pl.when(sec >= level)
        def _(level=level):
            @pl.when(sec > level)
            def _():
                if level > 0:
                    forward(4, level)
                arrive_rest(level)

            if level + 1 < levels:
                @pl.when(sec > level + 1)
                def _():
                    arrive_reduce(level + 1)

            take_halo(level, 0)

            @pl.loop(0, tiles)
            def _(m):
                @pl.when(m + 1 < tiles)
                def _():
                    take_halo(level, m + 1)

                finish_tile(level, m)
                if level + 1 < levels:
                    @pl.when(sec > level)
                    def _():
                        reduce_tile(level + 1, m)

            @pl.loop(0, tiles)
            def _(m):
                to_side(level, m).wait_send()
                for way in range(2):
                    @pl.when(has[1 - way])
                    def _(way=way):
                        to_strip(level, m, way).wait_send()

                    @pl.when(has[way])
                    def _(way=way):
                        pass_on(level, m, way).wait_send()

    for piece in range(6):
        for target in range(1, levels):
            @pl.when(sec < target)
            def _(piece=piece, target=target):
                across(piece, sec, target).wait_send()
        if piece < 5:
            for level in range(levels - 1):
                @pl.when(sec > level)
                def _(piece=piece, level=level):
                    for step in range(1, groups):
                        to_group(piece, level, step).wait_send()
                    for step in range(groups):
                        to_core(piece, level, col, step).wait_send()


def on_device(levels, strips, groups, x_in, w_reduce, w_spatial, w_expand, gain_mid, bias_mid, gain_out, bias_out):
    tiles, chans, rows, cols = x_in.shape
    mid = w_reduce.shape[1]
    operands = (
        x_in.reshape(tiles, chans * rows, cols), w_reduce[0], w_spatial[0], w_expand[0],
        gain_mid[0], bias_mid[0], gain_out.reshape(chans // mid, mid), bias_out.reshape(chans // mid, mid),
    )
    dma = pltpu.SemaphoreType.DMA
    out = pl.pallas_call(
        functools.partial(kernel, levels, strips, groups, rows),
        out_shape=jax.ShapeDtypeStruct((tiles, chans * rows, cols), F32),
        in_specs=[pl.BlockSpec(memory_space=pltpu.HBM)] * 8,
        out_specs=pl.BlockSpec(memory_space=pltpu.VMEM),
        scratch_shapes=[
            pltpu.VMEM((levels, mid, chans), F32),
            pltpu.VMEM((levels, 9, mid, mid), F32),
            pltpu.VMEM((levels, chans, mid), F32),
            pltpu.VMEM((levels, 4 + 2 * (chans // mid), mid), F32),
            pltpu.VMEM((levels, tiles, rows, mid, cols), F32),
            pltpu.VMEM((levels, tiles, rows, mid, cols), F32),
            pltpu.VMEM((levels, tiles, 2, mid, cols), F32),
            pltpu.VMEM((levels, tiles, 2, mid, cols), F32),
            pltpu.VMEM((levels, 2 * mid, chans), BF),
            pltpu.VMEM((levels, 2 * mid, 9 * mid), BF),
            pltpu.VMEM((levels, chans, 3 * mid), BF),
            pltpu.VMEM((levels, mid, cols), F32),
            pltpu.VMEM((levels, mid, cols), F32),
            pltpu.VMEM((levels, chans, cols), F32),
            pltpu.VMEM((6 * mid, (rows + 2) * cols), BF),
            pltpu.VMEM((2 * mid, rows * cols), BF),
            dma((tiles,)),
            dma((7,)),
            dma((6, levels)),
            dma((6, levels)),
            dma((5, levels, groups)),
            dma((5, levels, groups)),
            dma((5, levels, groups)),
            dma((5, levels, groups)),
            dma((levels, tiles, 2)),
            dma((levels, tiles, 2)),
            dma((levels, tiles)),
            dma((levels, tiles)),
            dma((levels, tiles, 2)),
            dma((levels, tiles, 2)),
        ],
        compiler_params=pltpu.CompilerParams(
            collective_id=0, has_side_effects=True, vmem_limit_bytes=40 * 1024 * 1024
        ),
        name="blocks",
    )(*(pltpu.with_memory_space_constraint(value, pltpu.HBM) for value in operands))
    return out.reshape(1, tiles, chans, rows, cols)


def solution(mesh):
    in_specs = (
        P("groups", None, "strip", "col"),
        P("section", None, None),
        P("section", None, None, None),
        P("section", None, None),
        P("section", None, None),
        P("section", None, None),
        P("section", None),
        P("section", None),
    )
    out_specs = P("section", "groups", None, "strip", "col")
    return jax.shard_map(
        functools.partial(on_device, mesh.shape["section"], mesh.shape["strip"], mesh.shape["groups"]),
        mesh=mesh, in_specs=in_specs, out_specs=out_specs, check_vma=False,
    )
```

```python
import functools

import jax
import jax.numpy as jnp
from jax import lax
from jax.experimental import pallas as pl
from jax.experimental.pallas import tpu as pltpu
from jax.sharding import PartitionSpec as P

BF = jnp.bfloat16
F32 = jnp.float32


def split(value):
    high = value.astype(BF)
    return high, (value - high.astype(F32)).astype(BF)


def dot(a, b):
    return jnp.dot(a, b, preferred_element_type=F32)


def down_rows(row, size):
    return jnp.transpose(jnp.broadcast_to(row, (size, size)))


def kernel(
    levels, strips, groups, rows,
    x_ref, wr_ref, ws_ref, wx_ref, gm_ref, bm_ref, go_ref, bo_ref, cur,
    wr_all, ws_all, wx_all, pp_all, red, edges, side, halo, corner, relay,
    w_red, w_spa, w_exp, b_red, b_mid, b_out, sa, middle,
    x_sem, own_sem, wsend, wrecv, gsend, grecv, rsend, rrecv, hsend, hrecv, nsend, nrecv, ysend, yrecv,
):
    tiles = x_ref.shape[0]
    chans = x_ref.shape[1] // rows
    cols = x_ref.shape[2]
    mid = wr_ref.shape[0]
    strip = lax.axis_index("strip")
    sec = lax.axis_index("section")
    col = lax.axis_index("col")
    grp = lax.axis_index("groups")
    other = {"col": 1 - col}
    srcs = (wr_ref, ws_ref, wx_ref)
    count = chans // mid
    terms = ((gm_ref, 0, 2), (bm_ref, 2, 2), (go_ref, 4, count), (bo_ref, 4 + count, count))
    slots = (wr_all, ws_all, wx_all, pp_all)

    def share(piece, level, which, of):
        part = which * groups + of
        if piece == 0:
            size = mid // (2 * groups)
            return wr_all.at[level, pl.ds(part * size, size), :]
        if piece < 4:
            size = mid // (2 * groups)
            return ws_all.at[level, pl.ds(3 * (piece - 1), 3), pl.ds(part * size, size), :]
        if piece == 4:
            size = chans // (2 * groups)
            return wx_all.at[level, pl.ds(part * size, size), :]
        return pp_all.at[level]

    def remote(src, dst, send, recv, device):
        return pltpu.make_async_remote_copy(
            src_ref=src, dst_ref=dst, send_sem=send, recv_sem=recv,
            device_id=device, device_id_type=pl.DeviceIdType.MESH,
        )

    def across(piece, level, target):
        part = share(piece, level, col, grp)
        return remote(
            part, part, wsend.at[piece, target], wrecv.at[piece, level], {"section": target}
        )

    def to_group(piece, level, step):
        part = share(piece, level, col, grp)
        return remote(
            part, part, gsend.at[piece, level, step], grecv.at[piece, level, step],
            {"groups": lax.rem(grp + step, groups)},
        )

    def to_core(piece, level, which, step):
        part = share(piece, level, which, lax.rem(grp + groups - step, groups))
        return remote(part, part, rsend.at[piece, level, step], rrecv.at[piece, level, step], other)

    def forward(piece, level):
        across(piece, level, 0).wait_recv()
        if piece < 5:
            for step in range(1, groups):
                to_group(piece, level, step).start()
            to_core(piece, level, col, 0).start()

    def collect(piece, level):
        for step in range(1, groups):
            part = share(piece, level, col, lax.rem(grp + groups - step, groups))
            remote(
                part, part, gsend.at[piece, level, step], grecv.at[piece, level, step], other
            ).wait_recv()
            to_core(piece, level, col, step).start()

    def complete(piece, level):
        for step in range(groups):
            to_core(piece, level, 1 - col, step).wait_recv()

    own = [
        pltpu.make_async_copy(srcs[k], slots[k].at[sec], own_sem.at[k]) for k in range(3)
    ] + [
        [
            pltpu.make_async_copy(src, pp_all.at[sec, pl.ds(first, size), :], own_sem.at[3 + i])
            for i, (src, first, size) in enumerate(terms)
        ]
    ]
    loads = [
        pltpu.make_async_copy(x_ref.at[m], cur.at[m], x_sem.at[m]) for m in range(tiles)
    ]
    for copy in (*own[3], own[0], own[1], own[2]):
        copy.start()
    for copy in loads:
        copy.start()

    barrier = pltpu.get_barrier_semaphore()
    pl.semaphore_signal(barrier, inc=1, device_id=other, device_id_type=pl.DeviceIdType.MESH)
    for step in range(1, levels):
        pl.semaphore_signal(
            barrier, inc=1, device_id={"section": lax.rem(sec + step, levels)},
            device_id_type=pl.DeviceIdType.MESH,
        )

    for there, peer in ((strip > 0, strip - 1), (strip < strips - 1, strip + 1)):
        @pl.when(there)
        def _(peer=peer):
            pl.semaphore_signal(
                barrier, inc=1, device_id={"strip": peer}, device_id_type=pl.DeviceIdType.MESH
            )

    for step in range(1, groups):
        pl.semaphore_signal(
            barrier, inc=1, device_id={"groups": lax.rem(grp + step, groups)},
            device_id_type=pl.DeviceIdType.MESH,
        )

    peers = levels + groups - 1 + jnp.where(strip > 0, 1, 0) + jnp.where(strip < strips - 1, 1, 0)
    pl.semaphore_wait(barrier, peers)

    for piece in (5, 0, 1, 2, 3, 4):
        for copy in {5: own[3], 0: own[:1], 1: own[1:2], 4: own[2:3]}.get(piece, ()):
            copy.wait()
        for target in range(1, levels):
            @pl.when(sec < target)
            def _(piece=piece, target=target):
                across(piece, sec, target).start()

    @pl.when(strip == 0)
    def _():
        halo[:, :, 0] = jnp.zeros(halo.shape[:2] + halo.shape[3:], F32)

    @pl.when(strip == strips - 1)
    def _():
        halo[:, :, 1] = jnp.zeros(halo.shape[:2] + halo.shape[3:], F32)

    def prepare_reduce(level):
        gain = down_rows(pp_all[level, 0:1, :], mid)
        for at in range(count):
            cut = slice(at * mid, (at + 1) * mid)
            high, low = split(wr_all[level, :, cut] * gain)
            w_red[level, 0:mid, cut] = high
            w_red[level, mid : 2 * mid, cut] = low
        b_red[level] = down_rows(pp_all[level, 2:3, :], mid)

    def prepare_spatial(level):
        gain = down_rows(pp_all[level, 1:2, :], mid)
        for tap in range(9):
            high, low = split(ws_all[level, tap] * gain)
            w_spa[level, 0:mid, tap * mid : (tap + 1) * mid] = high
            w_spa[level, mid : 2 * mid, tap * mid : (tap + 1) * mid] = low
        b_mid[level] = down_rows(pp_all[level, 3:4, :], mid)

    def prepare_expand(level):
        for at in range(count):
            cut = slice(at * mid, (at + 1) * mid)
            high, low = split(wx_all[level, cut, :] * down_rows(pp_all[level, pl.ds(4 + at, 1), :], mid))
            w_exp[level, cut, 0:mid] = high
            w_exp[level, cut, mid : 2 * mid] = high
            w_exp[level, cut, 2 * mid : 3 * mid] = low
            b_out[level, cut, :] = down_rows(pp_all[level, pl.ds(4 + count + at, 1), :], mid)

    def arrive_reduce(level):
        for piece in (5, 0, 1, 2):
            forward(piece, level)
        collect(0, level)
        forward(3, level)
        complete(0, level)
        prepare_reduce(level)

    def arrive_rest(level):
        for piece in (1, 2, 3):
            collect(piece, level)
        for piece in (1, 2, 3):
            complete(piece, level)
        prepare_spatial(level)
        collect(4, level)
        complete(4, level)
        prepare_expand(level)

    def to_strip(level, m, way):
        return remote(
            red.at[level, m, rows - 1 if way == 0 else 0], halo.at[level, m, way],
            hsend.at[level, m, way], hrecv.at[level, m, way],
            {"strip": strip + 1 if way == 0 else strip - 1},
        )

    def to_side(level, m):
        return remote(edges.at[level, m], side.at[level, m], nsend.at[level, m], nrecv.at[level, m], other)

    def pass_on(level, m):
        return remote(corner.at[level, m], relay.at[level, m], ysend.at[level, m], yrecv.at[level, m], other)

    lane = lax.broadcasted_iota(jnp.int32, (mid, cols), 1)
    on_edge = lane == jnp.where(col == 0, cols - 1, 0)

    def pack(values):
        total = jnp.where(on_edge, values[0], 0.0)
        for step, value in enumerate(values[1:], 1):
            total = total + pltpu.roll(jnp.where(on_edge, value, 0.0), step, 1)
        return total

    def unpack(value, step):
        return pltpu.roll(value, cols - step, 1) if step else value

    has = (strip > 0, strip < strips - 1)

    def reduce_tile(level, m):
        weights = w_red[level]
        bias = b_red[level]
        for pair in range(rows // 2):
            parts = [
                split(cur.at[m][pl.ds(2 * pair + j, chans, stride=rows), :]) for j in range(2)
            ]
            high = jnp.concatenate([part[0] for part in parts], axis=1)
            low = jnp.concatenate([part[1] for part in parts], axis=1)
            both = dot(weights, high)
            total = both[:mid] + both[mid:] + dot(weights[:mid], low)
            for j in range(2):
                red[level, m, 2 * pair + j] = jnp.maximum(total[:, j * cols : (j + 1) * cols] + bias, 0.0)

        @pl.when(has[1])
        def _():
            to_strip(level, m, 0).start()

        @pl.when(has[0])
        def _():
            to_strip(level, m, 1).start()

        edges[level, m] = pack([red[level, m, at] for at in range(rows)])
        to_side(level, m).start()

    def take_halo(level, m):
        for way in range(2):
            @pl.when(has[way])
            def _(way=way):
                to_strip(level, m, way).wait_recv()

        corner[level, m] = pack([halo[level, m, 0], halo[level, m, 1]])
        pass_on(level, m).start()

    left_edge = lane == cols - 1
    right_edge = lane == 0
    left_on = jnp.where(col == 1, 1.0, 0.0).astype(F32)
    right_on = jnp.where(col == 0, 1.0, 0.0).astype(F32)

    def finish_tile(level, m):
        to_side(level, m).wait_recv()
        pass_on(level, m).wait_recv()
        for at in range(rows + 2):
            if at == 0:
                centre, beside = halo[level, m, 0], relay[level, m]
            elif at == rows + 1:
                centre, beside = halo[level, m, 1], unpack(relay[level, m], 1)
            else:
                centre, beside = red[level, m, at - 1], unpack(side[level, m], at - 1)
            lanes = slice(at * cols, (at + 1) * cols)
            left = pltpu.roll(jnp.where(left_edge, beside * left_on, centre), 1, 1)
            right = pltpu.roll(jnp.where(right_edge, beside * right_on, centre), cols - 1, 1)
            for q, value in enumerate((left, centre, right)):
                high, low = split(value)
                sa[q * mid : (q + 1) * mid, lanes] = high
                sa[(3 + q) * mid : (4 + q) * mid, lanes] = low
        wide = rows * cols
        high, low = (
            jnp.concatenate(
                [sa[first : first + 3 * mid, p * cols : p * cols + wide] for p in range(3)], axis=0
            )
            for first in (0, 3 * mid)
        )
        both = dot(w_spa[level], high)
        total = both[:mid] + both[mid:] + dot(w_spa[level, 0:mid, :], low)
        total = jnp.maximum(total + jnp.concatenate([b_mid[level]] * rows, axis=1), 0.0)
        high, low = split(total)
        middle[0:mid, :] = high
        middle[mid : 2 * mid, :] = low
        for pair in range(rows // 2):
            lanes = slice(2 * pair * cols, (2 * pair + 2) * cols)
            high, low = middle[0:mid, lanes], middle[mid : 2 * mid, lanes]
            grown = dot(w_exp[level], jnp.concatenate([high, low, high], axis=0))
            for j in range(2):
                at = pl.ds(2 * pair + j, chans, stride=rows)
                cur.at[m][at, :] = jnp.maximum(
                    cur.at[m][at, :] + grown[:, j * cols : (j + 1) * cols] + b_out[level], 0.0
                )

    prepare_reduce(sec)

    @pl.when(sec > 0)
    def _():
        prepare_spatial(sec)
        prepare_expand(sec)
        arrive_reduce(0)

    @pl.loop(0, tiles)
    def _(m):
        pltpu.make_async_copy(x_ref.at[m], cur.at[m], x_sem.at[m]).wait()
        reduce_tile(0, m)

        @pl.when((sec > 0) & (m == 0))
        def _():
            forward(4, 0)

    @pl.when(sec == 0)
    def _():
        prepare_spatial(0)
        prepare_expand(0)

    for level in range(levels):
        @pl.when(sec >= level)
        def _(level=level):
            @pl.when(sec > level)
            def _():
                if level > 0:
                    forward(4, level)
                arrive_rest(level)

            if level + 1 < levels:
                @pl.when(sec > level + 1)
                def _():
                    arrive_reduce(level + 1)

            take_halo(level, 0)

            @pl.loop(0, tiles)
            def _(m):
                @pl.when(m + 1 < tiles)
                def _():
                    take_halo(level, m + 1)

                finish_tile(level, m)
                if level + 1 < levels:
                    @pl.when(sec > level)
                    def _():
                        reduce_tile(level + 1, m)

            @pl.loop(0, tiles)
            def _(m):
                to_side(level, m).wait_send()
                pass_on(level, m).wait_send()
                for way in range(2):
                    @pl.when(has[1 - way])
                    def _(way=way):
                        to_strip(level, m, way).wait_send()

    for piece in range(6):
        for target in range(1, levels):
            @pl.when(sec < target)
            def _(piece=piece, target=target):
                across(piece, sec, target).wait_send()
        if piece < 5:
            for level in range(levels - 1):
                @pl.when(sec > level)
                def _(piece=piece, level=level):
                    for step in range(1, groups):
                        to_group(piece, level, step).wait_send()
                    for step in range(groups):
                        to_core(piece, level, col, step).wait_send()


def on_device(levels, strips, groups, x_in, w_reduce, w_spatial, w_expand, gain_mid, bias_mid, gain_out, bias_out):
    tiles, chans, rows, cols = x_in.shape
    mid = w_reduce.shape[1]
    operands = (
        x_in.reshape(tiles, chans * rows, cols), w_reduce[0], w_spatial[0], w_expand[0],
        gain_mid[0], bias_mid[0], gain_out.reshape(chans // mid, mid), bias_out.reshape(chans // mid, mid),
    )
    dma = pltpu.SemaphoreType.DMA
    out = pl.pallas_call(
        functools.partial(kernel, levels, strips, groups, rows),
        out_shape=jax.ShapeDtypeStruct((tiles, chans * rows, cols), F32),
        in_specs=[pl.BlockSpec(memory_space=pltpu.HBM)] * 8,
        out_specs=pl.BlockSpec(memory_space=pltpu.VMEM),
        scratch_shapes=[
            pltpu.VMEM((levels, mid, chans), F32),
            pltpu.VMEM((levels, 9, mid, mid), F32),
            pltpu.VMEM((levels, chans, mid), F32),
            pltpu.VMEM((levels, 4 + 2 * (chans // mid), mid), F32),
            pltpu.VMEM((levels, tiles, rows, mid, cols), F32),
            pltpu.VMEM((levels, tiles, mid, cols), F32),
            pltpu.VMEM((levels, tiles, mid, cols), F32),
            pltpu.VMEM((levels, tiles, 2, mid, cols), F32),
            pltpu.VMEM((levels, tiles, mid, cols), F32),
            pltpu.VMEM((levels, tiles, mid, cols), F32),
            pltpu.VMEM((levels, 2 * mid, chans), BF),
            pltpu.VMEM((levels, 2 * mid, 9 * mid), BF),
            pltpu.VMEM((levels, chans, 3 * mid), BF),
            pltpu.VMEM((levels, mid, cols), F32),
            pltpu.VMEM((levels, mid, cols), F32),
            pltpu.VMEM((levels, chans, cols), F32),
            pltpu.VMEM((6 * mid, (rows + 2) * cols), BF),
            pltpu.VMEM((2 * mid, rows * cols), BF),
            dma((tiles,)),
            dma((7,)),
            dma((6, levels)),
            dma((6, levels)),
            dma((5, levels, groups)),
            dma((5, levels, groups)),
            dma((5, levels, groups)),
            dma((5, levels, groups)),
            dma((levels, tiles, 2)),
            dma((levels, tiles, 2)),
            dma((levels, tiles)),
            dma((levels, tiles)),
            dma((levels, tiles)),
            dma((levels, tiles)),
        ],
        compiler_params=pltpu.CompilerParams(
            collective_id=0, has_side_effects=True, vmem_limit_bytes=40 * 1024 * 1024
        ),
        name="blocks",
    )(*(pltpu.with_memory_space_constraint(value, pltpu.HBM) for value in operands))
    return out.reshape(1, tiles, chans, rows, cols)


def solution(mesh):
    in_specs = (
        P("groups", None, "strip", "col"),
        P("section", None, None),
        P("section", None, None, None),
        P("section", None, None),
        P("section", None, None),
        P("section", None, None),
        P("section", None),
        P("section", None),
    )
    out_specs = P("section", "groups", None, "strip", "col")
    return jax.shard_map(
        functools.partial(on_device, mesh.shape["section"], mesh.shape["strip"], mesh.shape["groups"]),
        mesh=mesh, in_specs=in_specs, out_specs=out_specs, check_vma=False,
    )
```

```python
import functools

import jax
import jax.numpy as jnp
from jax import lax
from jax.experimental import pallas as pl
from jax.experimental.pallas import tpu as pltpu
from jax.sharding import PartitionSpec as P

BF = jnp.bfloat16
F32 = jnp.float32


def split(value):
    high = value.astype(BF)
    return high, (value - high.astype(F32)).astype(BF)


def dot(a, b):
    return jnp.dot(a, b, preferred_element_type=F32)


def down_rows(row, size):
    return jnp.transpose(jnp.broadcast_to(row, (size, size)))


def kernel(
    levels, strips, groups, rows,
    x_ref, wr_ref, ws_ref, wx_ref, gm_ref, bm_ref, go_ref, bo_ref, cur,
    wr_all, ws_all, wx_all, pp_all, red, side, halo, relay,
    w_red, w_spa, w_exp, b_red, b_mid, b_out, sa, middle,
    x_sem, own_sem, wsend, wrecv, gsend, grecv, rsend, rrecv, hsend, hrecv, nsend, nrecv, ysend, yrecv,
):
    tiles = x_ref.shape[0]
    chans = x_ref.shape[1] // rows
    cols = x_ref.shape[2]
    mid = wr_ref.shape[0]
    strip = lax.axis_index("strip")
    sec = lax.axis_index("section")
    col = lax.axis_index("col")
    grp = lax.axis_index("groups")
    other = {"col": 1 - col}
    srcs = (wr_ref, ws_ref, wx_ref)
    count = chans // mid
    terms = ((gm_ref, 0, 2), (bm_ref, 2, 2), (go_ref, 4, count), (bo_ref, 4 + count, count))
    slots = (wr_all, ws_all, wx_all, pp_all)

    def share(piece, level, which, of):
        part = which * groups + of
        if piece == 0:
            size = mid // (2 * groups)
            return wr_all.at[level, pl.ds(part * size, size), :]
        if piece < 4:
            size = mid // (2 * groups)
            return ws_all.at[level, pl.ds(3 * (piece - 1), 3), pl.ds(part * size, size), :]
        if piece == 4:
            size = chans // (2 * groups)
            return wx_all.at[level, pl.ds(part * size, size), :]
        return pp_all.at[level]

    def remote(src, dst, send, recv, device):
        return pltpu.make_async_remote_copy(
            src_ref=src, dst_ref=dst, send_sem=send, recv_sem=recv,
            device_id=device, device_id_type=pl.DeviceIdType.MESH,
        )

    def across(piece, level, target):
        part = share(piece, level, col, grp)
        return remote(
            part, part, wsend.at[piece, target], wrecv.at[piece, level], {"section": target}
        )

    def to_group(piece, level, step):
        part = share(piece, level, col, grp)
        return remote(
            part, part, gsend.at[piece, level, step], grecv.at[piece, level, step],
            {"groups": lax.rem(grp + step, groups)},
        )

    def to_core(piece, level, which, step):
        part = share(piece, level, which, lax.rem(grp + groups - step, groups))
        return remote(part, part, rsend.at[piece, level, step], rrecv.at[piece, level, step], other)

    def forward(piece, level):
        across(piece, level, 0).wait_recv()
        if piece < 5:
            for step in range(1, groups):
                to_group(piece, level, step).start()
            to_core(piece, level, col, 0).start()

    def collect(piece, level):
        for step in range(1, groups):
            part = share(piece, level, col, lax.rem(grp + groups - step, groups))
            remote(
                part, part, gsend.at[piece, level, step], grecv.at[piece, level, step], other
            ).wait_recv()
            to_core(piece, level, col, step).start()

    def complete(piece, level):
        for step in range(groups):
            to_core(piece, level, 1 - col, step).wait_recv()

    own = [
        pltpu.make_async_copy(srcs[k], slots[k].at[sec], own_sem.at[k]) for k in range(3)
    ] + [
        [
            pltpu.make_async_copy(src, pp_all.at[sec, pl.ds(first, size), :], own_sem.at[3 + i])
            for i, (src, first, size) in enumerate(terms)
        ]
    ]
    loads = [
        pltpu.make_async_copy(x_ref.at[m], cur.at[m], x_sem.at[m]) for m in range(tiles)
    ]
    for copy in (*own[3], own[0], own[1], own[2]):
        copy.start()
    for copy in loads:
        copy.start()

    barrier = pltpu.get_barrier_semaphore()
    pl.semaphore_signal(barrier, inc=1, device_id=other, device_id_type=pl.DeviceIdType.MESH)
    for step in range(1, levels):
        pl.semaphore_signal(
            barrier, inc=1, device_id={"section": lax.rem(sec + step, levels)},
            device_id_type=pl.DeviceIdType.MESH,
        )

    for there, peer in ((strip > 0, strip - 1), (strip < strips - 1, strip + 1)):
        @pl.when(there)
        def _(peer=peer):
            pl.semaphore_signal(
                barrier, inc=1, device_id={"strip": peer}, device_id_type=pl.DeviceIdType.MESH
            )

    for step in range(1, groups):
        pl.semaphore_signal(
            barrier, inc=1, device_id={"groups": lax.rem(grp + step, groups)},
            device_id_type=pl.DeviceIdType.MESH,
        )

    peers = levels + groups - 1 + jnp.where(strip > 0, 1, 0) + jnp.where(strip < strips - 1, 1, 0)
    pl.semaphore_wait(barrier, peers)

    for piece in (5, 0, 1, 2, 3, 4):
        for copy in {5: own[3], 0: own[:1], 1: own[1:2], 4: own[2:3]}.get(piece, ()):
            copy.wait()
        for target in range(1, levels):
            @pl.when(sec < target)
            def _(piece=piece, target=target):
                across(piece, sec, target).start()

    @pl.when(strip == 0)
    def _():
        halo[:, :, 0] = jnp.zeros(halo.shape[:2] + halo.shape[3:], F32)
        relay[:, :, 0] = jnp.zeros(relay.shape[:2] + relay.shape[3:], F32)

    @pl.when(strip == strips - 1)
    def _():
        halo[:, :, 1] = jnp.zeros(halo.shape[:2] + halo.shape[3:], F32)
        relay[:, :, 1] = jnp.zeros(relay.shape[:2] + relay.shape[3:], F32)

    def prepare_reduce(level):
        gain = down_rows(pp_all[level, 0:1, :], mid)
        for at in range(count):
            cut = slice(at * mid, (at + 1) * mid)
            high, low = split(wr_all[level, :, cut] * gain)
            w_red[level, 0:mid, cut] = high
            w_red[level, mid : 2 * mid, cut] = low
        b_red[level] = down_rows(pp_all[level, 2:3, :], mid)

    def prepare_spatial(level):
        gain = down_rows(pp_all[level, 1:2, :], mid)
        for tap in range(9):
            high, low = split(ws_all[level, tap] * gain)
            w_spa[level, 0:mid, tap * mid : (tap + 1) * mid] = high
            w_spa[level, mid : 2 * mid, tap * mid : (tap + 1) * mid] = low
        b_mid[level] = down_rows(pp_all[level, 3:4, :], mid)

    def prepare_expand(level):
        for at in range(count):
            cut = slice(at * mid, (at + 1) * mid)
            high, low = split(wx_all[level, cut, :] * down_rows(pp_all[level, pl.ds(4 + at, 1), :], mid))
            w_exp[level, cut, 0:mid] = high
            w_exp[level, cut, mid : 2 * mid] = high
            w_exp[level, cut, 2 * mid : 3 * mid] = low
            b_out[level, cut, :] = down_rows(pp_all[level, pl.ds(4 + count + at, 1), :], mid)

    def arrive_reduce(level):
        for piece in (5, 0, 1, 2):
            forward(piece, level)
        collect(0, level)
        forward(3, level)
        complete(0, level)
        prepare_reduce(level)

    def arrive_rest(level):
        for piece in (1, 2, 3):
            collect(piece, level)
        for piece in (1, 2, 3):
            complete(piece, level)
        prepare_spatial(level)
        collect(4, level)
        complete(4, level)
        prepare_expand(level)

    def to_strip(level, m, way):
        return remote(
            red.at[level, m, rows - 1 if way == 0 else 0], halo.at[level, m, way],
            hsend.at[level, m, way], hrecv.at[level, m, way],
            {"strip": strip + 1 if way == 0 else strip - 1},
        )

    def to_side(level, m):
        return remote(red.at[level, m], side.at[level, m], nsend.at[level, m], nrecv.at[level, m], other)

    def pass_on(level, m, way):
        return remote(
            halo.at[level, m, way], relay.at[level, m, way],
            ysend.at[level, m, way], yrecv.at[level, m, way], other,
        )

    has = (strip > 0, strip < strips - 1)

    def reduce_tile(level, m):
        weights = w_red[level]
        bias = b_red[level]
        for pair in range(rows // 2):
            parts = [
                split(cur.at[m][pl.ds(2 * pair + j, chans, stride=rows), :]) for j in range(2)
            ]
            high = jnp.concatenate([part[0] for part in parts], axis=1)
            low = jnp.concatenate([part[1] for part in parts], axis=1)
            both = dot(weights, high)
            total = both[:mid] + both[mid:] + dot(weights[:mid], low)
            for j in range(2):
                red[level, m, 2 * pair + j] = jnp.maximum(total[:, j * cols : (j + 1) * cols] + bias, 0.0)

        @pl.when(has[1])
        def _():
            to_strip(level, m, 0).start()

        @pl.when(has[0])
        def _():
            to_strip(level, m, 1).start()

        to_side(level, m).start()

    def take_halo(level, m):
        for way in range(2):
            @pl.when(has[way])
            def _(way=way):
                to_strip(level, m, way).wait_recv()
                pass_on(level, m, way).start()

    lane = lax.broadcasted_iota(jnp.int32, (mid, cols), 1)
    left_edge = lane == cols - 1
    right_edge = lane == 0
    left_on = jnp.where(col == 1, 1.0, 0.0).astype(F32)
    right_on = jnp.where(col == 0, 1.0, 0.0).astype(F32)

    def finish_tile(level, m):
        to_side(level, m).wait_recv()
        for way in range(2):
            @pl.when(has[way])
            def _(way=way):
                pass_on(level, m, way).wait_recv()
        for at in range(rows + 2):
            if at == 0:
                centre, beside = halo[level, m, 0], relay[level, m, 0]
            elif at == rows + 1:
                centre, beside = halo[level, m, 1], relay[level, m, 1]
            else:
                centre, beside = red[level, m, at - 1], side[level, m, at - 1]
            lanes = slice(at * cols, (at + 1) * cols)
            left = pltpu.roll(jnp.where(left_edge, beside * left_on, centre), 1, 1)
            right = pltpu.roll(jnp.where(right_edge, beside * right_on, centre), cols - 1, 1)
            for q, value in enumerate((left, centre, right)):
                high, low = split(value)
                sa[q * mid : (q + 1) * mid, lanes] = high
                sa[(3 + q) * mid : (4 + q) * mid, lanes] = low
        wide = rows * cols
        high, low = (
            jnp.concatenate(
                [sa[first : first + 3 * mid, p * cols : p * cols + wide] for p in range(3)], axis=0
            )
            for first in (0, 3 * mid)
        )
        both = dot(w_spa[level], high)
        total = both[:mid] + both[mid:] + dot(w_spa[level, 0:mid, :], low)
        total = jnp.maximum(total + jnp.concatenate([b_mid[level]] * rows, axis=1), 0.0)
        high, low = split(total)
        middle[0:mid, :] = high
        middle[mid : 2 * mid, :] = low

        @pl.when(m + 1 < tiles)
        def _():
            take_halo(level, m + 1)

        for pair in range(rows // 2):
            lanes = slice(2 * pair * cols, (2 * pair + 2) * cols)
            high, low = middle[0:mid, lanes], middle[mid : 2 * mid, lanes]
            grown = dot(w_exp[level], jnp.concatenate([high, low, high], axis=0))
            for j in range(2):
                at = pl.ds(2 * pair + j, chans, stride=rows)
                cur.at[m][at, :] = jnp.maximum(
                    cur.at[m][at, :] + grown[:, j * cols : (j + 1) * cols] + b_out[level], 0.0
                )

    prepare_reduce(sec)

    @pl.when(sec > 0)
    def _():
        prepare_spatial(sec)
        prepare_expand(sec)
        arrive_reduce(0)

    @pl.loop(0, tiles)
    def _(m):
        pltpu.make_async_copy(x_ref.at[m], cur.at[m], x_sem.at[m]).wait()
        reduce_tile(0, m)

        @pl.when((sec > 0) & (m == 0))
        def _():
            forward(4, 0)

    @pl.when(sec == 0)
    def _():
        prepare_spatial(0)
        prepare_expand(0)

    for level in range(levels):
        @pl.when(sec >= level)
        def _(level=level):
            @pl.when(sec > level)
            def _():
                if level > 0:
                    forward(4, level)
                arrive_rest(level)

            if level + 1 < levels:
                @pl.when(sec > level + 1)
                def _():
                    arrive_reduce(level + 1)

            take_halo(level, 0)

            @pl.loop(0, tiles)
            def _(m):
                finish_tile(level, m)
                if level + 1 < levels:
                    @pl.when(sec > level)
                    def _():
                        reduce_tile(level + 1, m)

            @pl.loop(0, tiles)
            def _(m):
                to_side(level, m).wait_send()
                for way in range(2):
                    @pl.when(has[1 - way])
                    def _(way=way):
                        to_strip(level, m, way).wait_send()

                    @pl.when(has[way])
                    def _(way=way):
                        pass_on(level, m, way).wait_send()

    for piece in range(6):
        for target in range(1, levels):
            @pl.when(sec < target)
            def _(piece=piece, target=target):
                across(piece, sec, target).wait_send()
        if piece < 5:
            for level in range(levels - 1):
                @pl.when(sec > level)
                def _(piece=piece, level=level):
                    for step in range(1, groups):
                        to_group(piece, level, step).wait_send()
                    for step in range(groups):
                        to_core(piece, level, col, step).wait_send()


def on_device(levels, strips, groups, x_in, w_reduce, w_spatial, w_expand, gain_mid, bias_mid, gain_out, bias_out):
    tiles, chans, rows, cols = x_in.shape
    mid = w_reduce.shape[1]
    operands = (
        x_in.reshape(tiles, chans * rows, cols), w_reduce[0], w_spatial[0], w_expand[0],
        gain_mid[0], bias_mid[0], gain_out.reshape(chans // mid, mid), bias_out.reshape(chans // mid, mid),
    )
    dma = pltpu.SemaphoreType.DMA
    out = pl.pallas_call(
        functools.partial(kernel, levels, strips, groups, rows),
        out_shape=jax.ShapeDtypeStruct((tiles, chans * rows, cols), F32),
        in_specs=[pl.BlockSpec(memory_space=pltpu.HBM)] * 8,
        out_specs=pl.BlockSpec(memory_space=pltpu.VMEM),
        scratch_shapes=[
            pltpu.VMEM((levels, mid, chans), F32),
            pltpu.VMEM((levels, 9, mid, mid), F32),
            pltpu.VMEM((levels, chans, mid), F32),
            pltpu.VMEM((levels, 4 + 2 * (chans // mid), mid), F32),
            pltpu.VMEM((levels, tiles, rows, mid, cols), F32),
            pltpu.VMEM((levels, tiles, rows, mid, cols), F32),
            pltpu.VMEM((levels, tiles, 2, mid, cols), F32),
            pltpu.VMEM((levels, tiles, 2, mid, cols), F32),
            pltpu.VMEM((levels, 2 * mid, chans), BF),
            pltpu.VMEM((levels, 2 * mid, 9 * mid), BF),
            pltpu.VMEM((levels, chans, 3 * mid), BF),
            pltpu.VMEM((levels, mid, cols), F32),
            pltpu.VMEM((levels, mid, cols), F32),
            pltpu.VMEM((levels, chans, cols), F32),
            pltpu.VMEM((6 * mid, (rows + 2) * cols), BF),
            pltpu.VMEM((2 * mid, rows * cols), BF),
            dma((tiles,)),
            dma((7,)),
            dma((6, levels)),
            dma((6, levels)),
            dma((5, levels, groups)),
            dma((5, levels, groups)),
            dma((5, levels, groups)),
            dma((5, levels, groups)),
            dma((levels, tiles, 2)),
            dma((levels, tiles, 2)),
            dma((levels, tiles)),
            dma((levels, tiles)),
            dma((levels, tiles, 2)),
            dma((levels, tiles, 2)),
        ],
        compiler_params=pltpu.CompilerParams(
            collective_id=0, has_side_effects=True, vmem_limit_bytes=40 * 1024 * 1024
        ),
        name="blocks",
    )(*(pltpu.with_memory_space_constraint(value, pltpu.HBM) for value in operands))
    return out.reshape(1, tiles, chans, rows, cols)


def solution(mesh):
    in_specs = (
        P("groups", None, "strip", "col"),
        P("section", None, None),
        P("section", None, None, None),
        P("section", None, None),
        P("section", None, None),
        P("section", None, None),
        P("section", None),
        P("section", None),
    )
    out_specs = P("section", "groups", None, "strip", "col")
    return jax.shard_map(
        functools.partial(on_device, mesh.shape["section"], mesh.shape["strip"], mesh.shape["groups"]),
        mesh=mesh, in_specs=in_specs, out_specs=out_specs, check_vma=False,
    )
```
